32 devices in a mesh: grp: 4 (over y, x), dp: 8 (over z, core).
Axes of the slice: x: 2, y: 2, z: 4, core: 2. Of those that a mesh axis runs over, the one named last changes fastest.
Arguments:
- byte_tokens: int32 [32, 2, 128], P(('grp', 'dp')), may hold values from 0 to 383
- seg_lengths: int32 [32, 2, 3], P(('grp', 'dp')), may hold values from 1 to 64, 128 in all within a row
- scripts: int32 [32, 2, 3], P(('grp', 'dp')), may hold values from 0 to 2
- routes: int32 [32, 2, 128, 1], P(('grp', 'dp')), may hold values from 0 to 7; in each aligned block of 128 rows (0 to 127, 128 to 255, ..., all dimensions but the last counted through in order) at most 24 rows name the same one
- step_count: int32 [1], replicated, may hold values from 2 to 20
- attention_in: float32 [3, 1536, 2304], P(None, 'dp'), may hold values from -0.15625 to 0.15625
- attention_out: float32 [3, 768, 1536], P(None, 'dp'), may hold values from -1.25 to 1.25
- feed_in: float32 [2, 1536, 7936], P(None, 'dp'), may hold values from -0.15625 to 0.15625
- feed_out: float32 [2, 3968, 1536], P(None, 'dp'), may hold values from -0.09375 to 0.09375
- embedding: float32 [384, 1536], P('dp'), may hold values from -6 to 6
- norm_gains: float32 [7, 1536], P(None, 'dp'), may hold values from 0.5 to 1.5
- first_attention_in: float32 [3, 1536, 2304], P(None, 'dp'), may hold values from -9.536743e-07 to 9.536743e-07
- first_attention_out: float32 [3, 768, 1536], P(None, 'dp'), may hold values from -9.536743e-07 to 9.536743e-07
- first_feed_in: float32 [2, 1536, 7936], P(None, 'dp'), may hold values from -9.536743e-07 to 9.536743e-07
- first_feed_out: float32 [2, 3968, 1536], P(None, 'dp'), may hold values from -9.536743e-07 to 9.536743e-07
- first_embedding: float32 [384, 1536], P('dp'), may hold values from -9.536743e-07 to 9.536743e-07
- first_norm_gains: float32 [7, 1536], P(None, 'dp'), may hold values from -9.536743e-07 to 9.536743e-07
- second_attention_in: float32 [3, 1536, 2304], P(None, 'dp'), may hold values from 9.741758e-16 to 1.5586812e-14
- second_attention_out: float32 [3, 768, 1536], P(None, 'dp'), may hold values from 9.741758e-16 to 1.5586812e-14
- second_feed_in: float32 [2, 1536, 7936], P(None, 'dp'), may hold values from 9.741758e-16 to 1.5586812e-14
- second_feed_out: float32 [2, 3968, 1536], P(None, 'dp'), may hold values from 9.741758e-16 to 1.5586812e-14
- second_embedding: float32 [384, 1536], P('dp'), may hold values from 9.741758e-16 to 1.5586812e-14
- second_norm_gains: float32 [7, 1536], P(None, 'dp'), may hold values from 9.741758e-16 to 1.5586812e-14
Outputs:
- new_attention_in: float32 [3, 1536, 2304], P(None, 'dp')
- new_attention_out: float32 [3, 768, 1536], P(None, 'dp')
- new_feed_in: float32 [2, 1536, 7936], P(None, 'dp')
- new_feed_out: float32 [2, 3968, 1536], P(None, 'dp')
- new_embedding: float32 [384, 1536], P('dp')
- new_norm_gains: float32 [7, 1536], P(None, 'dp')
- new_first_attention_in: float32 [3, 1536, 2304], P(None, 'dp')
- new_first_attention_out: float32 [3, 768, 1536], P(None, 'dp')
- new_first_feed_in: float32 [2, 1536, 7936], P(None, 'dp')
- new_first_feed_out: float32 [2, 3968, 1536], P(None, 'dp')
- new_first_embedding: float32 [384, 1536], P('dp')
- new_first_norm_gains: float32 [7, 1536], P(None, 'dp')
- new_second_attention_in: float32 [3, 1536, 2304], P(None, 'dp')
- new_second_attention_out: float32 [3, 768, 1536], P(None, 'dp')
- new_second_feed_in: float32 [2, 1536, 7936], P(None, 'dp')
- new_second_feed_out: float32 [2, 3968, 1536], P(None, 'dp')
- new_second_embedding: float32 [384, 1536], P('dp')
- new_second_norm_gains: float32 [7, 1536], P(None, 'dp')
- mean_loss: float32 [], replicated
- script_counts: float32 [3], replicated
- gradient_norm: float32 [], replicated
The draws below stay inside these ranges and needn't reach their ends.
Inputs may be any that keep to these rules, and one draw needn't show every extreme that they name: `routes`: in each device's micro-batch at most 24 encoder rows name one decoder device, and some decoder device is named by exactly 24. `seg_lengths`: the 3 lengths of one device's micro-batch sum to 128; the longest is 64.
All inputs are finite; a program needn't handle non-finite values.
Results may differ from the reference program's by a relative error of at most 0.003.
The reference program's roundings to bfloat16 on the way count: a program that leaves them out, or rounds other values in their place, can miss the bound.
Values may be sent and summed in bfloat16 or wider, within the bound.
No kernel may reach another device: no remote copies, remote signals or barrier semaphores. Data moves between devices by JAX's collectives and lax.ppermute only.
A program may use at most 896 MiB of HBM per device.

```python
import math
import jax
import jax.numpy as jnp
import numpy as np
from jax import lax

D = 1536
FF = 3968
HEADS = 12
HEAD_DIM = 64
VOCAB = 384
INNER = 768
TOK = 128
SEQ = 3
MB = 2
CAP = 24
NPARAM = 51325440
N_GRP = 4
N_DP = 8


def with_ends(array, rng, smallest, top_value):
    longest = array.shape.index(max(array.shape))
    spots = []
    for shift in (0, 1):
        where = [jax.random.randint(jax.random.fold_in(rng, axis), (), 0, length) for axis, length in enumerate(array.shape)]
        where[longest] = (where[longest] + shift) % array.shape[longest]
        spots.append(tuple(where))
    return array.at[spots[0]].set(smallest).at[spots[1]].set(top_value)


def levels(own_key, extent, shards, least, largest):
    def one(dim, parts):
        draws = jax.random.uniform(jax.random.fold_in(jax.random.fold_in(own_key, 6), dim), (parts,), jnp.float32, least / len(shards), largest / len(shards))
        return jnp.repeat(jnp.exp(draws), extent[dim] // parts).reshape((-1,) + (1,) * (len(extent) - dim - 1))

    level = one(*shards[0])
    for cut in shards[1:]:
        level = level * one(*cut)
    return level


def rank_table(amount, skew):
    portions = [(1 << 20) // math.isqrt(rank ** skew) + 1 for rank in range(1, amount + 1)]
    spread = 1 + sum(portions) // (1 << 30)
    return np.cumsum(np.array([max(1, weight // spread) for weight in portions]))


def ranked_ids(own_key, dims, count, slope):
    table = rank_table(count, slope)
    ticket = jax.random.randint(jax.random.fold_in(own_key, 1), dims, 0, int(table[count - 1]))
    grade = jnp.searchsorted(jnp.asarray(table, jnp.int32), ticket, side="right")
    return jax.random.permutation(jax.random.fold_in(own_key, 2), count)[grade].astype(jnp.int32)


def profile(number_of, total, bound, skew):
    weights = [(1 << 20) // math.isqrt(rank ** skew) + 1 for rank in range(2, number_of + 1)]
    surplus, given = total - bound - (number_of - 1), [1] * (number_of - 1)
    while surplus > 0:
        movable = [i for i in range(number_of - 1) if given[i] < bound]
        whole, remaining = sum([weights[i] for i in movable]), surplus
        for i in movable:
            more = min(bound - given[i], max(1, remaining * weights[i] // whole), surplus)
            given[i] = given[i] + more
            surplus = surplus - more
    return np.array([bound] + given)


def ragged(key, amount, total, reach, lean):
    if amount == 2:
        one = jax.random.randint(key, (), max(1, total - reach), min(reach, total - 1) + 1)
        return jnp.stack([one, total - one])
    tallies = jnp.asarray(profile(amount, total, reach, lean), jnp.int32)
    twos = (amount - 1) // 2
    donor, receiver = tallies[1:1 + 2 * twos:2], tallies[2:2 + 2 * twos:2]
    room = jnp.minimum(donor - 1, reach - receiver)
    passed = jax.random.randint(jax.random.fold_in(key, 1), (twos,), 0, 1 << 20) % (room + 1)
    tallies = tallies.at[1:1 + 2 * twos:2].set(donor - passed).at[2:2 + 2 * twos:2].set(receiver + passed)
    return tallies[jax.random.permutation(jax.random.fold_in(key, 2), amount)]


def routed_block(key, own, number, rows, count, top, bound, slope):
    ranking = jax.random.permutation(key, count)
    crowded, ordinary = portions_of(count, rows * top, bound, slope, True), portions_of(count, rows * top, bound, slope, False)
    places = jnp.arange(count)

    def named(sizes, rotation):
        used = int((sizes > 0).sum())
        fixed = max(1, used // 4)
        moved = fixed + (places - fixed + rotation * (used - fixed)) % max(1, count - fixed)
        return jnp.zeros((count,), jnp.int32).at[ranking[jnp.where(places < fixed, places, moved)]].set(jnp.asarray(sizes, jnp.int32))

    sizes = jnp.where(number % 4 == 0, named(crowded, number // 4), named(ordinary, number - number // 4 - 1))
    mixed = jax.random.permutation(jax.random.fold_in(own, 3), count)
    source_of, taker = mixed[0:count // 2 * 2:2], mixed[1:count // 2 * 2:2]
    room = jnp.minimum(sizes[source_of] - 1, bound - sizes[taker]) // 2
    room = jnp.where((source_of == ranking[0]) | (taker == ranking[0]) | (sizes[taker] == 0), 0, jnp.maximum(room, 0))
    moved = jax.random.randint(jax.random.fold_in(own, 4), (count // 2,), 0, 1 << 20) % (room + 1)
    sizes = sizes.at[source_of].add(-moved).at[taker].add(moved)
    members = jnp.searchsorted(jnp.cumsum(sizes), jnp.arange(rows * top), side="right").astype(jnp.int32)
    listing = members.reshape(top, rows).T
    listing = listing[jax.random.permutation(jax.random.fold_in(own, 1), rows)]
    rotation = jax.random.randint(jax.random.fold_in(own, 2), (rows, 1), 0, top)
    return jnp.take_along_axis(listing, (jnp.arange(top)[None, :] + rotation) % top, axis=1)


def portions_of(amount, total, most, slope, full):
    portions = [(1 << 20) // math.isqrt(rank ** slope) + 1 for rank in range(1, amount + 1)]
    largest = most if full else min(most, max(-(-total // amount), total * portions[0] // sum(portions)))
    least = 1 if total - largest >= amount - 1 else 0
    given, spare = [largest] + [least] * (amount - 1), total - largest - least * (amount - 1)
    while spare > 0:
        free = [i for i in range(1, amount) if given[i] < largest] or [i for i in range(1, amount) if given[i] < most]
        pool, remaining = sum([portions[i] for i in free]), spare
        for i in free:
            extra = min(most - given[i], max(1, remaining * portions[i] // pool), spare)
            given[i] = given[i] + extra
            spare = spare - extra
    return np.array(given)


def centred(own_key, dims, deviation, bound, shards=(), held_as=jnp.bfloat16):
    array = deviation * jax.random.normal(own_key, dims, jnp.float32)
    if shards:
        array = array * levels(own_key, dims, shards, -0.22, 0.18)
    return jnp.clip(array, -bound, bound).astype(held_as)


def setup_inputs(seed: int = 0) -> dict:
    streams_of = jax.random.split(jax.random.key(seed), 24)
    byte_tokens = with_ends(ranked_ids(streams_of[0], (N_GRP * N_DP, MB, TOK), VOCAB, 2), jax.random.fold_in(streams_of[0], 3), 0, VOCAB - 1).astype(jnp.int32)
    seg_lengths = jax.vmap(lambda own: ragged(own, SEQ, TOK, TOK // 2, 2))(jax.random.split(streams_of[1], (N_GRP * N_DP) * MB)).reshape((N_GRP * N_DP, MB, SEQ)).astype(jnp.int32)
    scripts = with_ends(jax.random.randint(streams_of[2], (N_GRP * N_DP, MB, SEQ), 0, 3), jax.random.fold_in(streams_of[2], 1), 0, 2).astype(jnp.int32)
    routes_keys = jax.random.split(jax.random.fold_in(streams_of[3], 1), (N_GRP * N_DP) * MB * TOK // TOK)
    routes_turns = jax.random.permutation(jax.random.fold_in(streams_of[3], 3), (N_GRP * N_DP) * MB * TOK // TOK)
    routes = jax.vmap(lambda own, number: routed_block(jax.random.fold_in(streams_of[3], 2), own, number, TOK, N_DP, 1, CAP, 2))(routes_keys, routes_turns).reshape((N_GRP * N_DP, MB, TOK, 1))
    step_count = jax.random.randint(streams_of[4], (1,), 2, 21).astype(jnp.int32)
    attention_in = centred(streams_of[5], (3, D, 3 * INNER), D ** -0.5, 0.15625, ((1, 8),), jnp.float32)
    attention_out = centred(streams_of[6], (3, INNER, D), (max(4 * INNER // TOK, 1)) ** -0.5, 1.25, ((1, 8),), jnp.float32)
    feed_in = centred(streams_of[7], (2, D, 2 * FF), D ** -0.5, 0.15625, ((1, 8),), jnp.float32)
    feed_out = centred(streams_of[8], (2, FF, D), FF ** -0.5, 0.09375, ((1, 8),), jnp.float32)
    embedding = centred(streams_of[9], (VOCAB, D), 1.0, 6.0, ((0, 8),), jnp.float32)
    norm_gains = jnp.clip(1.0 + 0.1 * jax.random.normal(streams_of[10], (7, D), jnp.float32), 0.5, 1.5)
    first_attention_in = centred(streams_of[11], (3, D, 3 * INNER), (0.0011 / NPARAM ** 0.5), 9.5367431640625e-07, ((1, 8),), jnp.float32)
    first_attention_out = centred(streams_of[12], (3, INNER, D), (0.0011 / NPARAM ** 0.5), 9.5367431640625e-07, ((1, 8),), jnp.float32)
    first_feed_in = centred(streams_of[13], (2, D, 2 * FF), (0.0011 / NPARAM ** 0.5), 9.5367431640625e-07, ((1, 8),), jnp.float32)
    first_feed_out = centred(streams_of[14], (2, FF, D), (0.0011 / NPARAM ** 0.5), 9.5367431640625e-07, ((1, 8),), jnp.float32)
    first_embedding = centred(streams_of[15], (VOCAB, D), (0.0011 / NPARAM ** 0.5), 9.5367431640625e-07, ((0, 8),), jnp.float32)
    first_norm_gains = centred(streams_of[16], (7, D), (0.0011 / NPARAM ** 0.5), 9.5367431640625e-07, ((1, 8),), jnp.float32)
    second_attention_in = jnp.clip(jnp.exp(math.log(1.5586812304171568e-14) - 2.7725887 * jax.random.uniform(streams_of[17], (3, D, 3 * INNER), jnp.float32) ** levels(streams_of[17], (3, D, 3 * INNER), ((1, 8),), -0.2, 0.2)), 9.74175769010723e-16, 1.5586812304171568e-14)
    second_attention_out = jnp.clip(jnp.exp(math.log(1.5586812304171568e-14) - 2.7725887 * jax.random.uniform(streams_of[18], (3, INNER, D), jnp.float32) ** levels(streams_of[18], (3, INNER, D), ((1, 8),), -0.2, 0.2)), 9.74175769010723e-16, 1.5586812304171568e-14)
    second_feed_in = jnp.clip(jnp.exp(math.log(1.5586812304171568e-14) - 2.7725887 * jax.random.uniform(streams_of[19], (2, D, 2 * FF), jnp.float32) ** levels(streams_of[19], (2, D, 2 * FF), ((1, 8),), -0.2, 0.2)), 9.74175769010723e-16, 1.5586812304171568e-14)
    second_feed_out = jnp.clip(jnp.exp(math.log(1.5586812304171568e-14) - 2.7725887 * jax.random.uniform(streams_of[20], (2, FF, D), jnp.float32) ** levels(streams_of[20], (2, FF, D), ((1, 8),), -0.2, 0.2)), 9.74175769010723e-16, 1.5586812304171568e-14)
    second_embedding = jnp.clip(jnp.exp(math.log(1.5586812304171568e-14) - 2.7725887 * jax.random.uniform(streams_of[21], (VOCAB, D), jnp.float32) ** levels(streams_of[21], (VOCAB, D), ((0, 8),), -0.2, 0.2)), 9.74175769010723e-16, 1.5586812304171568e-14)
    second_norm_gains = jnp.clip(jnp.exp(math.log(1.5586812304171568e-14) - 2.7725887 * jax.random.uniform(streams_of[22], (7, D), jnp.float32) ** levels(streams_of[22], (7, D), ((1, 8),), -0.2, 0.2)), 9.74175769010723e-16, 1.5586812304171568e-14)
    return dict(byte_tokens=byte_tokens, seg_lengths=seg_lengths, scripts=scripts, routes=routes, step_count=step_count, attention_in=attention_in, attention_out=attention_out, feed_in=feed_in, feed_out=feed_out, embedding=embedding, norm_gains=norm_gains, first_attention_in=first_attention_in, first_attention_out=first_attention_out, first_feed_in=first_feed_in, first_feed_out=first_feed_out, first_embedding=first_embedding, first_norm_gains=first_norm_gains, second_attention_in=second_attention_in, second_attention_out=second_attention_out, second_feed_in=second_feed_in, second_feed_out=second_feed_out, second_embedding=second_embedding, second_norm_gains=second_norm_gains)


HIGH = lax.Precision.HIGHEST
NORM_EPS = 1e-06
MASKED = -1e+30
CLIP = 0.01
LEARN_RATE = 0.05
BETA_ONE = 0.9
BETA_TWO = 0.999
ADAM_EPS = 1e-08
DECAY = 0.01

@jax.custom_vjp
def low(v):
    return lax.optimization_barrier(v.astype(jnp.bfloat16)).astype(jnp.float32)

@jax.custom_vjp
def low_back(v):
    return v

def low_keep(v):
    return (low(v), None)

def low_pass(kept, grad):
    return (grad,)

def back_keep(v):
    return (v, None)

def back_low(kept, grad):
    return (low(grad),)
low.defvjp(low_keep, low_pass)
low_back.defvjp(back_keep, back_low)

def rounded(value):
    return low_back(low(value))

def product(left, right):
    return jnp.dot(left, right, precision=HIGH)

def root_norm(stream, gain):
    return stream * lax.rsqrt(lax.optimization_barrier(jnp.mean(stream * stream, -1, keepdims=True)) + NORM_EPS) * gain

def segment_of(lengths, row_count):
    bounds = jnp.cumsum(lengths)
    position = jnp.arange(row_count, dtype=jnp.int32)
    return lax.optimization_barrier(jnp.sum((position[:, None] >= bounds[None, :]).astype(jnp.int32), 1))

def softmax_rows(scores):
    row_max = lax.optimization_barrier(jnp.max(scores, -1, keepdims=True))
    raised = jnp.exp(scores - row_max)
    return raised / lax.optimization_barrier(jnp.sum(raised, -1, keepdims=True))

def attend(queries, keys, values, allowed):
    row_count = queries.shape[0]
    split_q = queries.reshape(row_count, HEADS, HEAD_DIM)
    split_k = keys.reshape(keys.shape[0], HEADS, HEAD_DIM)
    split_v = values.reshape(values.shape[0], HEADS, HEAD_DIM)
    scores = low_back(jnp.einsum('qhd,khd->hqk', split_q, split_k, precision=HIGH) * 0.125)
    shares = low(softmax_rows(jnp.where(allowed[None], scores, MASKED)))
    attended = jnp.einsum('hqk,khd->qhd', shares, split_v, precision=HIGH)
    return rounded(attended.reshape(row_count, INNER))

def attention_block(stream, gain, w_in, w_out, allowed):
    normed = low(root_norm(stream, gain))
    packed = rounded(product(normed, w_in))
    attended = attend(packed[:, :INNER], packed[:, INNER:2 * INNER], packed[:, 2 * INNER:], allowed)
    return stream + low_back(product(attended, w_out))

def feed_block(stream, gain, w_in, w_out):
    normed = low(root_norm(stream, gain))
    hidden = low_back(product(normed, w_in))
    gated = low(jax.nn.gelu(hidden[:, :FF], approximate=True) * hidden[:, FF:])
    return stream + low_back(product(gated, w_out))

def total_loss(params, byte_tokens, seg_lengths, scripts, routes, scale_kind):
    attn_in, attn_out, ffn_in, ffn_out, table, gains = [low(value) for value in params]
    encoders = (N_GRP - 1) * N_DP

    def encode(carry, item):
        tokens, lengths = item
        segment = segment_of(lengths, TOK)
        stream = jnp.take(table, tokens, axis=0)
        stream = attention_block(stream, gains[0], attn_in[0], attn_out[0], segment[:, None] == segment[None, :])
        stream = feed_block(stream, gains[1], ffn_in[0], ffn_out[0])
        return (carry, low(root_norm(stream, gains[2])))
    unused, states = lax.scan(jax.checkpoint(encode), jnp.float32(0.0), (byte_tokens[:encoders].reshape(-1, TOK), seg_lengths[:encoders].reshape(-1, SEQ)))
    states = states.reshape(encoders, MB, TOK, D).transpose(1, 0, 2, 3).reshape(MB, encoders * TOK, D)
    memory = rounded(jnp.einsum('bnd,de->bne', states, attn_in[2][:, INNER:], precision=HIGH))
    target = routes[:encoders, :, :, 0].transpose(1, 0, 2).reshape(MB, encoders * TOK)
    device_ids = jnp.repeat(jnp.arange(N_DP, dtype=jnp.int32), MB)
    micro_ids = jnp.tile(jnp.arange(MB, dtype=jnp.int32), N_DP)

    def decode(total, item):
        tokens, lengths, script_ids, device, micro = item
        segment = segment_of(lengths, TOK)
        position = jnp.arange(TOK, dtype=jnp.int32)
        starts = jnp.concatenate([jnp.ones((1,), bool), segment[1:] != segment[:-1]])
        previous = jnp.concatenate([jnp.zeros((1,), jnp.int32), tokens[:-1]])
        inputs = jnp.where(starts, 0, previous).astype(jnp.int32)
        stream = jnp.take(table, inputs, axis=0)
        causal = (segment[:, None] == segment[None, :]) & (position[None, :] <= position[:, None])
        stream = attention_block(stream, gains[3], attn_in[1], attn_out[1], causal)
        normed = low(root_norm(stream, gains[4]))
        queries = rounded(product(normed, attn_in[2][:, :INNER]))
        keys_values = lax.dynamic_index_in_dim(memory, micro, 0, keepdims=False)
        owners = lax.dynamic_index_in_dim(target, micro, 0, keepdims=False) == device
        allowed = jnp.broadcast_to(owners[None, :], (TOK, owners.shape[0]))
        attended = attend(queries, keys_values[:, :INNER], keys_values[:, INNER:], allowed)
        stream = stream + low_back(product(attended, attn_out[2]))
        stream = feed_block(stream, gains[5], ffn_in[1], ffn_out[1])
        head_in = low(root_norm(stream, gains[6]) * D ** (-0.5))
        logits = low_back(product(head_in, table.T))
        row_max = lax.optimization_barrier(jnp.max(logits, -1, keepdims=True))
        log_total = row_max[:, 0] + jnp.log(lax.optimization_barrier(jnp.sum(jnp.exp(logits - row_max), -1)))
        picked = lax.optimization_barrier(jnp.sum(jnp.where(jnp.arange(VOCAB)[None, :] == tokens[:, None], logits, 0.0), 1))
        token_kind = lax.optimization_barrier(jnp.sum(jnp.where(segment[:, None] == jnp.arange(SEQ)[None, :], script_ids[None, :], 0), 1))
        weight = lax.optimization_barrier(jnp.sum(jnp.where(token_kind[:, None] == jnp.arange(3)[None, :], scale_kind[None, :], 0.0), 1))
        return (total + jnp.sum((log_total - picked) * weight), None)
    items = (byte_tokens[encoders:].reshape(-1, TOK), seg_lengths[encoders:].reshape(-1, SEQ), scripts[encoders:].reshape(-1, SEQ), device_ids, micro_ids)
    loss_value, unused = lax.scan(jax.checkpoint(decode), jnp.float32(0.0), items)
    return loss_value

def optimizer_step(weight, first_moment, second, gradient, factor, step_value, decay):
    gradient = gradient * factor
    first_moment = BETA_ONE * first_moment + (1.0 - BETA_ONE) * gradient
    second = BETA_TWO * second + (1.0 - BETA_TWO) * gradient * gradient
    fixed_first = first_moment / (1.0 - BETA_ONE ** step_value)
    fixed_second = second / (1.0 - BETA_TWO ** step_value)
    weight = weight - LEARN_RATE * (fixed_first / (jnp.sqrt(fixed_second) + ADAM_EPS) + decay * weight)
    return (weight, first_moment, second)

def reference(byte_tokens, seg_lengths, scripts, routes, step_count, attention_in, attention_out, feed_in, feed_out, embedding, norm_gains, first_attention_in, first_attention_out, first_feed_in, first_feed_out, first_embedding, first_norm_gains, second_attention_in, second_attention_out, second_feed_in, second_feed_out, second_embedding, second_norm_gains):
    encoders = (N_GRP - 1) * N_DP
    kinds = scripts[encoders:]
    lengths = seg_lengths[encoders:]
    counts = lax.optimization_barrier(jnp.sum(jnp.where(kinds[..., None] == jnp.arange(3)[None, None, None, :], lengths[..., None], 0), (0, 1, 2))).astype(jnp.float32)
    scale_kind = 1.0 / (3.0 * jnp.maximum(counts, 1.0))
    params = (attention_in, attention_out, feed_in, feed_out, embedding, norm_gains)
    loss_value, pull = jax.vjp(lambda *values: total_loss(values, byte_tokens, seg_lengths, scripts, routes, scale_kind), *params)
    grads = pull(jnp.ones((), jnp.float32))
    norm = jnp.sqrt(sum((jnp.sum(gradient * gradient) for gradient in grads)))
    factor = jnp.minimum(1.0, CLIP / (norm + 1e-06))
    step_value = step_count[0].astype(jnp.float32)
    firsts = (first_attention_in, first_attention_out, first_feed_in, first_feed_out, first_embedding, first_norm_gains)
    seconds = (second_attention_in, second_attention_out, second_feed_in, second_feed_out, second_embedding, second_norm_gains)
    decays = (DECAY, DECAY, DECAY, DECAY, DECAY, 0.0)
    results = [optimizer_step(params[index], firsts[index], seconds[index], grads[index], factor, step_value, decays[index]) for index in range(6)]
    return (results[0][0], results[1][0], results[2][0], results[3][0], results[4][0], results[5][0], results[0][1], results[1][1], results[2][1], results[3][1], results[4][1], results[5][1], results[0][2], results[1][2], results[2][2], results[3][2], results[4][2], results[5][2], loss_value, counts, norm)
```

```python
import functools

import jax
import jax.numpy as jnp
from jax import lax
from jax.experimental import pallas as pl
from jax.experimental.pallas import tpu as pltpu
from jax.sharding import PartitionSpec as P

HEAD_DIM = 64
LANES = 128

LOW = jnp.bfloat16
FULL = jnp.float32
NORM_EPS = 1e-06
MASKED = -1e30
CLIP = 0.01
LEARN_RATE = 0.05
BETA_ONE = 0.9
BETA_TWO = 0.999
ADAM_EPS = 1e-08
DECAY = 0.01


def matmul(left, right):
    return jnp.dot(left, right, preferred_element_type=FULL)


def transposed_left(left, right):
    return lax.dot_general(left, right, (((0,), (0,)), ((), ())), preferred_element_type=FULL)


def transposed_right(left, right):
    return lax.dot_general(left, right, (((1,), (1,)), ((), ())), preferred_element_type=FULL)


def root_norm(stream, gain):
    return stream * lax.rsqrt(jnp.mean(stream * stream, -1, keepdims=True) + NORM_EPS) * gain


def root_norm_back(stream, gain, cotangent):
    unused, pull = jax.vjp(root_norm, stream, gain)
    return pull(cotangent)


def gate_apply(hidden):
    half_width = hidden.shape[1] // 2
    return jax.nn.gelu(hidden[:, :half_width], approximate=True) * hidden[:, half_width:]


def heads_of(matrix):
    return matrix.reshape(matrix.shape[0], matrix.shape[1], matrix.shape[2] // HEAD_DIM, HEAD_DIM)


def attend(queries, keys, values, allowed):
    scores = (
        jnp.einsum("bqhd,bkhd->bhqk", heads_of(queries), heads_of(keys), preferred_element_type=FULL)
        * 0.125
    )
    scores = jnp.where(allowed[:, None], scores, MASKED)
    row_max = jnp.max(scores, -1, keepdims=True)
    raised = jnp.exp(scores - row_max)
    shares = raised / jnp.sum(raised, -1, keepdims=True)
    attended = jnp.einsum(
        "bhqk,bkhd->bqhd", shares.astype(LOW), heads_of(values), preferred_element_type=FULL
    )
    return (attended.reshape(queries.shape).astype(LOW), shares)


def attend_back(queries, keys, values, shares, grad_attended):
    grad_heads = heads_of(grad_attended)
    grad_shares = jnp.einsum(
        "bqhd,bkhd->bhqk", grad_heads, heads_of(values), preferred_element_type=FULL
    )
    grad_scores = shares * (grad_shares - jnp.sum(shares * grad_shares, -1, keepdims=True))
    grad_low = (grad_scores * 0.125).astype(LOW)
    grad_q = jnp.einsum("bhqk,bkhd->bqhd", grad_low, heads_of(keys), preferred_element_type=FULL)
    grad_k = jnp.einsum("bhqk,bqhd->bkhd", grad_low, heads_of(queries), preferred_element_type=FULL)
    grad_v = jnp.einsum(
        "bhqk,bqhd->bkhd", shares.astype(LOW), grad_heads, preferred_element_type=FULL
    )
    return (
        grad_q.reshape(queries.shape).astype(LOW),
        grad_k.reshape(keys.shape).astype(LOW),
        grad_v.reshape(values.shape).astype(LOW),
    )


def adam(weight, first_moment, second, gradient, factor, fix_one, fix_two, decay):
    gradient = gradient * factor
    first_moment = BETA_ONE * first_moment + (1.0 - BETA_ONE) * gradient
    second = BETA_TWO * second + (1.0 - BETA_TWO) * gradient * gradient
    fixed_first = first_moment / fix_one
    fixed_second = second / fix_two
    weight = weight - LEARN_RATE * (
        fixed_first / (jnp.sqrt(fixed_second) + ADAM_EPS) + decay * weight
    )
    return (weight, first_moment, second)


def send(value, step, sources=None):
    groups = lax.axis_size("grp")
    sources = range(groups) if sources is None else sources
    return lax.ppermute(value, "grp", [(source, source ^ step) for source in sources])


def halves(value):
    middle = value.shape[1] // 2
    return value[:, :middle], value[:, middle:]


def gather_groups(value):
    rows = value.shape[0]
    left, right = halves(value)
    left_one = send(left, 1)
    right_two = send(right, 2)
    left_more = send(jnp.concatenate([left, left_one], 0), 2)
    right_more = send(jnp.concatenate([right, right_two], 0), 1)
    return jnp.concatenate(
        [
            jnp.concatenate([left, left_one, left_more], 0),
            jnp.concatenate([right, right_more[:rows], right_two, right_more[rows:]], 0),
        ],
        1,
    )


def reduce_groups(parts):
    rows = parts.shape[0] // 4
    left, right = halves(parts)
    left_low, right_low = left.astype(LOW), right.astype(LOW)
    got_left = send(left_low[2 * rows :], 2).astype(FULL)
    got_right = send(
        jnp.concatenate([right_low[rows : 2 * rows], right_low[3 * rows :]], 0), 1
    ).astype(FULL)
    more_left = send((left[rows : 2 * rows] + got_left[rows:]).astype(LOW), 1).astype(FULL)
    more_right = send((right[2 * rows : 3 * rows] + got_right[rows:]).astype(LOW), 2).astype(FULL)
    return jnp.concatenate(
        [left[:rows] + got_left[:rows] + more_left, right[:rows] + got_right[:rows] + more_right],
        1,
    )


def spread_last(value, is_last):
    last = lax.axis_size("grp") - 1
    left, right = halves(value)
    left_first = send(left, 1, [last])
    right_first = send(right, 2, [last])
    right_then = send(jnp.where(is_last, right, right_first), 1, [last, last ^ 2])
    left_then = send(jnp.where(is_last, left, left_first), 2, [last, last ^ 1])
    own = jnp.where(is_last, value, jnp.zeros_like(value))
    return own + jnp.concatenate([left_first + left_then, right_first + right_then], 1)


def collect_last(part):
    last = lax.axis_size("grp") - 1
    left, right = halves(part)
    left_first = send(left.astype(LOW), 2, [last ^ 3, last ^ 2]).astype(FULL)
    right_first = send(right.astype(LOW), 1, [last ^ 3, last ^ 1]).astype(FULL)
    left_then = send((left + left_first).astype(LOW), 1, [last ^ 1]).astype(FULL)
    right_then = send((right + right_first).astype(LOW), 2, [last ^ 2]).astype(FULL)
    return jnp.concatenate([left + left_first + left_then, right + right_first + right_then], 1)


def by_group(slots, group):
    return [
        lax.dynamic_index_in_dim(slots, group ^ source, 0, keepdims=False)
        for source in range(slots.shape[0])
    ]


def tie(value, *others):
    return lax.optimization_barrier((value,) + others)[0]


def deal_columns(feed_in, group, groups):
    layers, rows, width = feed_in.shape
    half = width // 2
    blocks = half // LANES
    own = -(-blocks // groups)

    def kernel(group_ref, source_ref, out_ref):
        place = pl.program_id(1) % own
        inside = groups * place + group_ref[0] < blocks
        out_ref[...] = jnp.where(inside, source_ref[...], 0.0).astype(LOW)

    def source_map(layer, step, group_ref):
        block = jnp.minimum(groups * (step % own) + group_ref[0], blocks - 1)
        return (layer, 0, (step // own) * blocks + block)

    return pl.pallas_call(
        kernel,
        out_shape=jax.ShapeDtypeStruct((layers, rows, 2 * own * LANES), LOW),
        grid_spec=pltpu.PrefetchScalarGridSpec(
            num_scalar_prefetch=1,
            grid=(layers, 2 * own),
            in_specs=[pl.BlockSpec((1, rows, LANES), source_map)],
            out_specs=pl.BlockSpec((1, rows, LANES), lambda layer, step, ref: (layer, 0, step)),
        ),
    )(group.reshape(1), feed_in)


class RowDeal:
    def __init__(self, shard_rows, members, groups):
        self.rows = shard_rows
        self.members = members
        self.groups = groups
        self.round = groups * LANES
        self.gap = self.round - shard_rows
        self.blocks = shard_rows * members // LANES
        self.own = -(-self.blocks // groups)
        self.snug = self.gap > 0 and self.gap * members == LANES and self.own == members

    def gather(self, shard, group, member):
        width = shard.shape[1]
        if not self.snug:
            whole = lax.all_gather(shard, "dp", axis=0, tiled=True)
            padded = jnp.pad(whole, ((0, self.own * self.round - whole.shape[0]), (0, 0)))
            dealt = padded.reshape(self.own, self.groups, LANES, width)
            picked = lax.dynamic_index_in_dim(dealt, group, 1, keepdims=False)
            return picked.reshape(self.own * LANES, width)
        padded = jnp.pad(shard, ((0, self.gap), (0, 0)))
        doubled = jnp.concatenate([padded, padded], 0)
        piece = lax.dynamic_slice(
            doubled, (self.gap * member + LANES * group, 0), (LANES, width)
        )
        held = lax.all_gather(piece, "dp", axis=0, tiled=False)
        after = jnp.concatenate([held[1:], jnp.zeros_like(held[:1])], 0)
        limit = (LANES - self.gap) - self.gap * jnp.arange(self.members)[:, None, None]
        place = jnp.arange(LANES)[None, :, None]
        wrapped = jnp.where(place < limit, held, after)
        return jnp.where(group == self.groups - 1, wrapped, held).reshape(-1, width)

    def arrange(self, grad, group):
        width = grad.shape[1]
        if not self.snug:
            spread = jnp.zeros((self.own, self.groups, LANES, width), grad.dtype)
            spread = lax.dynamic_update_index_in_dim(
                spread, grad.reshape(self.own, 1, LANES, width), group, 1
            )
            return spread.reshape(-1, width)[: self.rows * self.members]
        held = grad.reshape(self.members, LANES, width)
        before = jnp.concatenate([jnp.zeros_like(held[:1]), held[:-1]], 0)
        index = self.gap * jnp.arange(self.members)[:, None, None]
        place = jnp.arange(LANES)[None, :, None]
        wrapped = jnp.where(
            place < (LANES - self.gap) - index,
            held,
            jnp.where(place >= LANES - index, before, jnp.zeros_like(held)),
        )
        held = jnp.where(group == self.groups - 1, wrapped, held)
        return held.reshape(-1, width)

    def restore(self, parts, member):
        if not self.snug:
            return jnp.sum(parts, 0)
        width = parts.shape[2]
        line = parts.reshape(self.round, width)
        doubled = jnp.concatenate([line, line], 0)
        start = (self.round - self.gap * member) % self.round
        return lax.dynamic_slice(doubled, (start, 0), (self.rows, width))


def feed_in_step(weights, firsts, seconds, dealt, scalars, group):
    layers, rows, width = weights.shape
    groups = dealt[0].shape[0]
    blocks = width // LANES
    half_blocks = blocks // 2
    own = dealt[0].shape[2] // (2 * LANES)
    dealt = jnp.stack(dealt)

    def kernel(group_ref, scalar_ref, w_ref, m_ref, v_ref, *rest):
        grads, outs = rest[:groups], rest[groups:]
        for place in range(groups):
            lanes = slice(place * LANES, (place + 1) * LANES)
            gradient = grads[place][0, 0].astype(FULL)
            new = adam(
                w_ref[0, :, lanes],
                m_ref[0, :, lanes],
                v_ref[0, :, lanes],
                gradient,
                scalar_ref[0],
                scalar_ref[1],
                scalar_ref[2],
                DECAY,
            )
            for out, value in zip(outs, new):
                out[0, :, lanes] = value

    def grad_spec(place):
        def index(layer, step, group_ref, scalar_ref):
            block = jnp.minimum(step * groups + place, blocks - 1)
            part = (block >= half_blocks).astype(jnp.int32)
            block = block - part * half_blocks
            slot = jnp.bitwise_xor(group_ref[0], block % groups)
            return (layer, slot, 0, part * own + block // groups)

        return pl.BlockSpec((1, 1, rows, LANES), index)

    state_spec = pl.BlockSpec(
        (1, rows, groups * LANES), lambda layer, step, group_ref, scalar_ref: (layer, 0, step)
    )
    return pl.pallas_call(
        kernel,
        out_shape=[jax.ShapeDtypeStruct(weights.shape, FULL)] * 3,
        grid_spec=pltpu.PrefetchScalarGridSpec(
            num_scalar_prefetch=2,
            grid=(layers, -(-blocks // groups)),
            in_specs=[state_spec] * 3 + [grad_spec(place) for place in range(groups)],
            out_specs=[state_spec] * 3,
        ),
        cost_estimate=pl.CostEstimate(
            flops=20 * weights.size, bytes_accessed=26 * weights.size, transcendentals=weights.size
        ),
    )(group.reshape(1), scalars, weights, firsts, seconds, *([dealt] * groups))


def per_device(
    byte_tokens,
    seg_lengths,
    scripts,
    routes,
    step_count,
    attention_in,
    attention_out,
    feed_in,
    feed_out,
    embedding,
    norm_gains,
    first_attention_in,
    first_attention_out,
    first_feed_in,
    first_feed_out,
    first_embedding,
    first_norm_gains,
    second_attention_in,
    second_attention_out,
    second_feed_in,
    second_feed_out,
    second_embedding,
    second_norm_gains,
):
    groups = lax.axis_size("grp")
    members = lax.axis_size("dp")
    group = lax.axis_index("grp")
    member = lax.axis_index("dp")
    last = groups - 1
    is_decoder = group == last
    role = is_decoder.astype(jnp.int32)
    as_decoder = is_decoder.astype(FULL)
    decoder_slot = group ^ last
    micro, row_count = byte_tokens.shape[1:]
    tokens_here = micro * row_count
    shard_width = attention_in.shape[1]
    width = shard_width * members
    inner = attention_in.shape[2] // 3
    shard_inner = inner // members
    own_inner = inner // groups
    own_packed = 3 * own_inner
    own_width = width // groups
    shard_vocab = embedding.shape[0]
    vocab_size = shard_vocab * members
    capacity = 3 * row_count // (2 * members)
    slots = members * capacity
    deal = RowDeal(feed_out.shape[1], members, groups)
    scale_head = width ** (-0.5)

    tokens = byte_tokens[0]
    lengths = seg_lengths[0]
    bounds = jnp.cumsum(lengths, 1)
    position = jnp.arange(row_count, dtype=jnp.int32)
    segment = jnp.sum((position[None, :, None] >= bounds[:, None, :]).astype(jnp.int32), 2)
    same_row = segment[:, :, None] == segment[:, None, :]
    allowed_self = same_row & (
        jnp.logical_not(is_decoder) | (position[None, None, :] <= position[None, :, None])
    )
    starts = jnp.concatenate(
        [jnp.ones((micro, 1), bool), segment[:, 1:] != segment[:, :-1]], 1
    )
    previous = jnp.concatenate([jnp.zeros((micro, 1), jnp.int32), tokens[:, :-1]], 1)
    shifted = jnp.where(starts, 0, previous)
    inputs = jnp.where(is_decoder, shifted, tokens).reshape(tokens_here)
    target = routes[0, :, :, 0]
    hits = (target[:, :, None] == jnp.arange(members)[None, None, :]).astype(FULL)
    hits = hits * (1.0 - as_decoder)
    earlier = (position[:, None] > position[None, :]).astype(FULL)
    order = jnp.einsum("tu,bum->btm", earlier, hits, preferred_element_type=FULL)
    place = jnp.sum((order + capacity * jnp.arange(members, dtype=FULL)) * hits, 2)
    place = jnp.where(jnp.sum(hits, 2) > 0, place, -1.0)
    place = jnp.stack([place] + [send(place, step) for step in range(1, groups)])
    chosen = (
        place[..., None] == jnp.arange(slots, dtype=FULL)[None, None, None, :]
    ).astype(LOW)
    route_counts = jnp.sum(hits, 1)
    local_counts = (
        jnp.sum(
            jnp.where(scripts[0][..., None] == jnp.arange(3), lengths[..., None], 0), (0, 1)
        ).astype(FULL)
        * as_decoder
    )

    def pick(array):
        return lax.dynamic_index_in_dim(array, role, 0, keepdims=False).astype(LOW)

    def gather(value):
        return lax.all_gather(value, "dp", axis=0, tiled=True)

    def scatter(value):
        return lax.psum_scatter(value, "dp", scatter_dimension=0, tiled=True)

    extra = jnp.concatenate(
        [norm_gains.reshape(-1), local_counts, route_counts.reshape(-1)]
    ).astype(LOW)
    extra = jnp.pad(extra, (0, 8 * width - extra.shape[0])).reshape(8, width)
    packed_table = lax.all_gather(
        jnp.concatenate([embedding.astype(LOW), extra], 0), "dp", axis=0, tiled=False
    )
    table = packed_table[:, :shard_vocab].reshape(vocab_size, width)
    extras = packed_table[:, shard_vocab:].reshape(members, 8 * width)
    gain_size = 7 * shard_width
    gains = (
        extras[:, :gain_size].reshape(members, 7, shard_width).transpose(1, 0, 2).reshape(7, width)
    ).astype(FULL)
    counts = jnp.sum(extras[:, gain_size : gain_size + 3].astype(FULL), 0)
    scale_kind = 1.0 / (3.0 * jnp.maximum(counts, 1.0))
    came = extras[:, gain_size + 3 : gain_size + 3 + micro * members].astype(FULL)
    came = came.reshape(members, micro, members)
    came = lax.dynamic_index_in_dim(came, member, 2, keepdims=False)
    came = jnp.stack([came] + [send(came, step) for step in range(1, groups)])

    w_self_in = gather(pick(attention_in))

    onehot_inputs = (inputs[:, None] == jnp.arange(vocab_size)[None, :]).astype(LOW)
    stream0 = matmul(onehot_inputs, table)
    gain_self = jnp.where(is_decoder, gains[3], gains[0])
    normed_self = root_norm(stream0, gain_self).astype(LOW)
    packed_flat = matmul(normed_self, w_self_in).astype(LOW)
    w_self_out = gather(tie(pick(attention_out), table))
    dealt_in = deal_columns(tie(feed_in, table), group, groups)
    w_enc_in = gather(dealt_in[0])
    packed = packed_flat.reshape(micro, row_count, 3 * inner)
    q_self, k_self, v_self = (
        packed[:, :, :inner],
        packed[:, :, inner : 2 * inner],
        packed[:, :, 2 * inner :],
    )
    attended_self, shares_self = attend(q_self, k_self, v_self, allowed_self)
    attended_self = attended_self.reshape(tokens_here, inner)
    w_enc_out = deal.gather(tie(feed_out[0].astype(LOW), packed_flat), group, member)
    stream1 = stream0 + matmul(attended_self, w_self_out)

    gain_next = jnp.where(is_decoder, gains[4], gains[1])
    normed_next = root_norm(stream1, gain_next).astype(LOW)
    all_next = gather_groups(normed_next)
    cross_in = attention_in[2].reshape(shard_width, 3, groups, own_inner)
    own_cross = lax.dynamic_index_in_dim(cross_in, group, 2, keepdims=False)
    own_cross = own_cross.reshape(shard_width, own_packed).astype(LOW)
    w_cross = gather(tie(own_cross, normed_next))
    w_query, w_memory = w_cross[:, :own_inner], w_cross[:, own_inner:]
    w_cross_out = gather(tie(attention_out[2].astype(LOW), normed_next))
    w_dec_in = gather(tie(dealt_in[1], all_next))
    hidden_enc = matmul(all_next, w_enc_in)
    gated_enc = gate_apply(hidden_enc).astype(LOW)
    w_dec_out = deal.gather(tie(feed_out[1].astype(LOW), gated_enc), group, member)
    stream2e = stream1 + reduce_groups(matmul(gated_enc, w_enc_out))
    states = root_norm(stream2e, gains[2]).astype(LOW)
    all_states = gather_groups(states)
    memory_rows = matmul(all_states, w_memory).astype(LOW)

    def enter(slot):
        return slot + (slot >= decoder_slot).astype(jnp.int32)

    def enter_back(slot):
        return slot - (decoder_slot < slot).astype(jnp.int32)

    def reorder(array, places):
        return jnp.stack(
            [lax.dynamic_index_in_dim(array, index, 0, keepdims=False) for index in places]
        )

    encoder_slots = [enter(slot) for slot in range(last)]
    placed = jnp.einsum(
        "gbts,gbtd->gbsd",
        reorder(chosen, encoder_slots),
        reorder(memory_rows.reshape(groups, micro, row_count, 2 * own_inner), encoder_slots),
        preferred_element_type=FULL,
    ).astype(LOW)
    outgoing = placed.reshape(last, micro, members, capacity, 2 * own_inner)
    outgoing = outgoing.transpose(2, 1, 0, 3, 4)
    outgoing = outgoing.reshape(members, micro * last * capacity, 2 * own_inner)
    arrived = lax.all_to_all(outgoing, "dp", split_axis=0, concat_axis=0, tiled=True)
    key_count = members * last * capacity
    memory = arrived.reshape(members, micro, last * capacity, 2 * own_inner)
    memory = memory.transpose(1, 0, 2, 3).reshape(micro, key_count, 2 * own_inner)
    present = (
        jnp.arange(capacity, dtype=FULL)[None, None, None, :]
        < reorder(came, encoder_slots).transpose(2, 1, 0)[..., None]
    ).reshape(micro, key_count)
    allowed_cross = jnp.broadcast_to(present[:, None, :], (micro, row_count, key_count))

    cross_input = lax.dynamic_index_in_dim(
        all_next.reshape(groups, tokens_here, width), decoder_slot, 0, keepdims=False
    )
    queries = matmul(cross_input, w_query).astype(LOW).reshape(micro, row_count, own_inner)
    keys, values = memory[:, :, :own_inner], memory[:, :, own_inner:]
    attended_own, shares_cross = attend(queries, keys, values, allowed_cross)
    attended_own = attended_own.reshape(tokens_here, own_inner)
    attended_cross = jnp.concatenate(
        [send(attended_own, last ^ source, [source]) for source in range(last)] + [attended_own],
        1,
    )
    stream2d = stream1 + matmul(attended_cross, w_cross_out)

    all_dec = spread_last(root_norm(stream2d, gains[5]).astype(LOW), is_decoder)
    hidden_dec = matmul(all_dec, w_dec_in)
    gated_dec = gate_apply(hidden_dec).astype(LOW)
    stream3 = stream2d + collect_last(matmul(gated_dec, w_dec_out))

    head_in = (root_norm(stream3, gains[6]) * scale_head).astype(LOW)
    logits = transposed_right(head_in, table)
    row_max = jnp.max(logits, -1, keepdims=True)
    raised = jnp.exp(logits - row_max)
    row_total = jnp.sum(raised, -1, keepdims=True)
    flat_tokens = tokens.reshape(tokens_here)
    onehot_vocab = (jnp.arange(vocab_size)[None, :] == flat_tokens[:, None]).astype(FULL)
    log_total = row_max[:, 0] + jnp.log(row_total[:, 0])
    picked = jnp.sum(logits * onehot_vocab, 1)
    token_kind = jnp.sum(
        jnp.where(
            segment[:, :, None] == jnp.arange(lengths.shape[1])[None, None, :],
            scripts[0][:, None, :],
            0,
        ),
        2,
    ).reshape(tokens_here)
    weight = jnp.sum(
        jnp.where(token_kind[:, None] == jnp.arange(3)[None, :], scale_kind[None, :], 0.0), 1
    )
    weight = weight * as_decoder
    loss_part = jnp.sum((log_total - picked) * weight)
    grad_logits = ((raised / row_total - onehot_vocab) * weight[:, None]).astype(LOW)
    cotangent, gain_six = root_norm_back(
        stream3, gains[6], matmul(grad_logits, table) * scale_head
    )

    def feed_back(hidden, grad_all, w_in, w_out):
        unused, pull = jax.vjp(gate_apply, hidden)
        grad_hidden = pull(transposed_right(grad_all, w_out))[0].astype(LOW)
        return grad_hidden, transposed_right(grad_hidden, w_in)

    grad_all_dec = spread_last(cotangent.astype(LOW), is_decoder)
    grad_hidden_dec, part = feed_back(hidden_dec, grad_all_dec, w_dec_in, w_dec_out)
    grad_dec_in = transposed_left(all_dec, grad_hidden_dec).astype(LOW)
    grad_dec_out = deal.arrange(
        transposed_left(gated_dec, grad_all_dec).astype(LOW), group
    )
    collected, grad_dec_in, grad_dec_out = lax.optimization_barrier(
        (collect_last(part), grad_dec_in, grad_dec_out)
    )
    owned_dec_in = scatter(grad_dec_in)
    owned_dec_out = scatter(grad_dec_out)
    grad_stream, gain_five = root_norm_back(stream2d, gains[5], collected)
    cotangent = cotangent + grad_stream

    grad_low = cotangent.astype(LOW)
    grad_attended = transposed_right(grad_low, w_cross_out).astype(LOW)
    grad_own = jnp.where(is_decoder, grad_attended[:, last * own_inner :], 0)
    for source in range(last):
        grad_own = grad_own + send(
            grad_attended[:, source * own_inner : (source + 1) * own_inner], last ^ source, [last]
        )
    grad_q, grad_k, grad_v = attend_back(
        queries, keys, values, shares_cross, grad_own.reshape(micro, row_count, own_inner)
    )
    grad_memory = jnp.concatenate([grad_k, grad_v], 2)
    grad_memory = grad_memory.reshape(micro, members, last * capacity, 2 * own_inner)
    grad_memory = grad_memory.transpose(1, 0, 2, 3).reshape(outgoing.shape)
    reached = lax.all_to_all(grad_memory, "dp", split_axis=0, concat_axis=0, tiled=True)
    grad_q = grad_q.reshape(tokens_here, own_inner)
    grad_query_in = transposed_left(cross_input, grad_q)
    collected = collect_last(transposed_right(grad_q, w_query))
    grad_cross_out = transposed_left(attended_cross, grad_low).astype(LOW)
    grad_table = transposed_left(grad_logits, head_in)
    reached, grad_query_in, grad_cross_out, collected, grad_table = lax.optimization_barrier(
        (reached, grad_query_in, grad_cross_out, collected, grad_table)
    )
    owned_cross_out = scatter(grad_cross_out)
    reached = reached.reshape(members, micro, last, capacity, 2 * own_inner)
    reached = reached.transpose(2, 1, 0, 3, 4).reshape(last, micro, slots, 2 * own_inner)
    grad_rows = jnp.einsum(
        "gbts,gbsd->gbtd",
        chosen,
        reorder(reached, [jnp.minimum(enter_back(slot), last - 1) for slot in range(groups)]),
        preferred_element_type=FULL,
    )
    grad_rows = grad_rows.astype(LOW).reshape(groups * tokens_here, 2 * own_inner)
    grad_stream, gain_four = root_norm_back(stream1, gains[4], collected)
    cotangent_dec = cotangent + grad_stream

    reduced = reduce_groups(transposed_right(grad_rows, w_memory))
    grad_memory_in = transposed_left(all_states, grad_rows)
    reduced, grad_cross_in = lax.optimization_barrier(
        (reduced, jnp.concatenate([grad_query_in, grad_memory_in], 1))
    )
    owned_cross_in = scatter(grad_cross_in)
    cotangent_enc, gain_two = root_norm_back(stream2e, gains[2], reduced)
    grad_low = jnp.where(is_decoder, 0.0, cotangent_enc).astype(LOW)
    grad_all_enc = gather_groups(grad_low)
    grad_hidden_enc, part = feed_back(hidden_enc, grad_all_enc, w_enc_in, w_enc_out)
    grad_enc_in = transposed_left(all_next, grad_hidden_enc).astype(LOW)
    grad_enc_out = deal.arrange(
        transposed_left(gated_enc, grad_all_enc).astype(LOW), group
    )
    reduced, grad_enc_in, grad_enc_out = lax.optimization_barrier(
        (reduce_groups(part), grad_enc_in, grad_enc_out)
    )
    owned_enc_in = scatter(grad_enc_in)
    owned_enc_out = scatter(grad_enc_out)
    grad_stream, gain_one = root_norm_back(stream1, gains[1], reduced)
    cotangent_enc = cotangent_enc + grad_stream

    cotangent = jnp.where(is_decoder, cotangent_dec, cotangent_enc)
    grad_low = cotangent.astype(LOW)
    grad_attended = transposed_right(grad_low, w_self_out).astype(LOW)
    grads = attend_back(
        q_self, k_self, v_self, shares_self, grad_attended.reshape(micro, row_count, inner)
    )
    grad_packed = jnp.concatenate(grads, 2).reshape(tokens_here, 3 * inner)
    grad_stream, gain_zero = root_norm_back(
        stream0, gain_self, transposed_right(grad_packed, w_self_in)
    )
    cotangent = cotangent + grad_stream
    grad_lookup = lax.dot_general(
        onehot_inputs.astype(FULL),
        cotangent,
        (((0,), (0,)), ((), ())),
        precision=lax.Precision.HIGHEST,
        preferred_element_type=FULL,
    )
    grad_table = grad_table + grad_lookup

    all_normed, all_attended = (
        gather_groups(tie(normed_self, all_next)),
        gather_groups(tie(attended_self, all_next)),
    )

    def exchange_columns(value, columns):
        pieces = jnp.stack(
            [value[:, start : start + columns] for start in range(0, groups * columns, columns)]
        )
        mine = by_group(pieces, group)
        return jnp.concatenate(
            [mine[0]] + [send(mine[step], step) for step in range(1, groups)], 0
        )

    slot_of = (jnp.arange(groups * tokens_here) // tokens_here)[:, None]
    from_encoder = slot_of != decoder_slot

    def both_roles(left, right):
        right_slots = right.reshape(groups, tokens_here, -1)
        left_slots = left.reshape(groups, tokens_here, -1)
        return (
            transposed_left(left, jnp.where(from_encoder, right, 0)),
            transposed_left(
                lax.dynamic_index_in_dim(left_slots, decoder_slot, 0, keepdims=False),
                lax.dynamic_index_in_dim(right_slots, decoder_slot, 0, keepdims=False),
            ),
        )

    self_in_enc, self_in_dec = both_roles(all_normed, exchange_columns(grad_packed, own_packed))
    self_out_enc, self_out_dec = both_roles(all_attended, exchange_columns(grad_low, own_width))
    self_out = jnp.stack(
        [
            self_out_enc.reshape(members, shard_inner, own_width),
            self_out_dec.reshape(members, shard_inner, own_width),
        ],
        1,
    ).reshape(width, own_width)
    owned_self = scatter(jnp.concatenate([self_in_enc, self_in_dec, self_out], 1))

    encoder_only = 1.0 - as_decoder
    grad_gains = jnp.stack(
        [
            gain_zero * encoder_only,
            gain_one * encoder_only,
            gain_two * encoder_only,
            gain_zero * as_decoder,
            gain_four * as_decoder,
            gain_five * as_decoder,
            gain_six * as_decoder,
        ]
    )
    gain_rows = grad_gains.reshape(7, members, shard_width).transpose(1, 0, 2)
    gain_rows = gain_rows.reshape(members, gain_size)
    scalars = jnp.concatenate([loss_part[None], local_counts])
    gain_rows = jnp.concatenate(
        [gain_rows, jnp.broadcast_to(scalars[None], (members, 4))], 1
    )
    gain_rows = jnp.pad(gain_rows, ((0, 0), (0, 8 * width - gain_rows.shape[1])))
    last_pack = jnp.concatenate(
        [
            grad_table.reshape(members, shard_vocab, width),
            gain_rows.reshape(members, 8, width),
        ],
        1,
    )
    owned_pack = scatter(last_pack.reshape(members * (shard_vocab + 8), width))

    def every(value):
        return gather_groups(value).reshape((groups,) + value.shape)

    every_dec_in, every_dec_out = every(owned_dec_in), every(owned_dec_out)
    every_enc_in, every_enc_out = every(owned_enc_in), every(owned_enc_out)
    summed_pack = sum(by_group(every(owned_pack), group))
    grad_embedding = summed_pack[:shard_vocab]
    summed_rest = summed_pack[shard_vocab:].reshape(-1)
    grad_norm_gains = summed_rest[:gain_size].reshape(7, shard_width)
    loss_value = summed_rest[gain_size]
    total_counts = summed_rest[gain_size + 1 : gain_size + 4]
    cross_parts = by_group(every(owned_cross_in), group)
    self_parts = by_group(every(owned_self), group)
    final_cross_out = spread_last(owned_cross_out, is_decoder).astype(FULL)
    final_attention_in = jnp.stack(
        [
            jnp.concatenate([part[:, :own_packed] for part in self_parts], 1),
            jnp.concatenate([part[:, own_packed : 2 * own_packed] for part in self_parts], 1),
            jnp.concatenate(
                [
                    part[:, own_inner * kind : own_inner * (kind + 1)]
                    for kind in range(3)
                    for part in cross_parts
                ],
                1,
            ),
        ]
    )
    final_attention_out = jnp.stack(
        [
            jnp.concatenate([part[:shard_inner, 2 * own_packed :] for part in self_parts], 1),
            jnp.concatenate([part[shard_inner:, 2 * own_packed :] for part in self_parts], 1),
            final_cross_out,
        ]
    )
    final_feed_out = jnp.stack(
        [
            deal.restore(jnp.stack(by_group(parts, group)), member)
            for parts in (every_enc_out, every_dec_out)
        ]
    ).astype(FULL)

    def square(value):
        value = value.astype(FULL)
        return jnp.sum(value * value)

    first_group = (group == 0).astype(FULL)
    squares = (
        square(owned_enc_in)
        + square(owned_dec_in)
        + square(owned_enc_out)
        + square(owned_dec_out)
        + square(owned_cross_in)
        + square(owned_self)
        + as_decoder * square(owned_cross_out)
        + first_group * (square(grad_embedding) + square(grad_norm_gains))
    )
    norm = jnp.sqrt(lax.psum(squares, ("grp", "dp")))
    factor = jnp.minimum(1.0, CLIP / (norm + 1e-06))
    step_value = step_count[0].astype(FULL)
    fix_one = 1.0 - BETA_ONE**step_value
    fix_two = 1.0 - BETA_TWO**step_value
    new_feed_in = feed_in_step(
        feed_in,
        first_feed_in,
        second_feed_in,
        (every_enc_in, every_dec_in),
        jnp.stack([factor, fix_one, fix_two]),
        group,
    )

    def step(weight, first, second, gradient, decay):
        return adam(weight, first, second, gradient, factor, fix_one, fix_two, decay)

    results = [
        step(attention_in, first_attention_in, second_attention_in, final_attention_in, DECAY),
        step(attention_out, first_attention_out, second_attention_out, final_attention_out, DECAY),
        new_feed_in,
        step(feed_out, first_feed_out, second_feed_out, final_feed_out, DECAY),
        step(embedding, first_embedding, second_embedding, grad_embedding, DECAY),
        step(norm_gains, first_norm_gains, second_norm_gains, grad_norm_gains, 0.0),
    ]
    return (
        *(result[0] for result in results),
        *(result[1] for result in results),
        *(result[2] for result in results),
        loss_value,
        total_counts,
        norm,
    )


def solution(mesh):
    weights = (
        P(None, "dp", None),
        P(None, "dp", None),
        P(None, "dp", None),
        P(None, "dp", None),
        P("dp", None),
        P(None, "dp"),
    )
    in_specs = (
        P(("grp", "dp"), None, None),
        P(("grp", "dp"), None, None),
        P(("grp", "dp"), None, None),
        P(("grp", "dp"), None, None, None),
        P(),
    ) + 3 * weights
    out_specs = 3 * weights + (P(), P(), P())
    return jax.shard_map(
        per_device, mesh=mesh, in_specs=in_specs, out_specs=out_specs, check_vma=False
    )
```

```python
import functools

import jax
import jax.numpy as jnp
from jax import lax
from jax.experimental import pallas as pl
from jax.experimental.pallas import tpu as pltpu
from jax.sharding import PartitionSpec as P

HEAD_DIM = 64
LANES = 128

LOW = jnp.bfloat16
FULL = jnp.float32
NORM_EPS = 1e-06
MASKED = -1e30
CLIP = 0.01
LEARN_RATE = 0.05
BETA_ONE = 0.9
BETA_TWO = 0.999
ADAM_EPS = 1e-08
DECAY = 0.01


def matmul(left, right):
    return jnp.dot(left, right, preferred_element_type=FULL)


def transposed_left(left, right):
    return lax.dot_general(left, right, (((0,), (0,)), ((), ())), preferred_element_type=FULL)


def transposed_right(left, right):
    return lax.dot_general(left, right, (((1,), (1,)), ((), ())), preferred_element_type=FULL)


def root_norm(stream, gain):
    return stream * lax.rsqrt(jnp.mean(stream * stream, -1, keepdims=True) + NORM_EPS) * gain


def root_norm_back(stream, gain, cotangent):
    unused, pull = jax.vjp(root_norm, stream, gain)
    return pull(cotangent)


def gate_apply(hidden):
    half_width = hidden.shape[1] // 2
    return jax.nn.gelu(hidden[:, :half_width], approximate=True) * hidden[:, half_width:]


def heads_of(matrix):
    return matrix.reshape(matrix.shape[0], matrix.shape[1], matrix.shape[2] // HEAD_DIM, HEAD_DIM)


def attend(queries, keys, values, allowed):
    scores = (
        jnp.einsum("bqhd,bkhd->bhqk", heads_of(queries), heads_of(keys), preferred_element_type=FULL)
        * 0.125
    )
    scores = jnp.where(allowed[:, None], scores, MASKED)
    row_max = jnp.max(scores, -1, keepdims=True)
    raised = jnp.exp(scores - row_max)
    shares = raised / jnp.sum(raised, -1, keepdims=True)
    attended = jnp.einsum(
        "bhqk,bkhd->bqhd", shares.astype(LOW), heads_of(values), preferred_element_type=FULL
    )
    return (attended.reshape(queries.shape).astype(LOW), shares)


def attend_back(queries, keys, values, shares, grad_attended):
    grad_heads = heads_of(grad_attended)
    grad_shares = jnp.einsum(
        "bqhd,bkhd->bhqk", grad_heads, heads_of(values), preferred_element_type=FULL
    )
    grad_scores = shares * (grad_shares - jnp.sum(shares * grad_shares, -1, keepdims=True))
    grad_low = (grad_scores * 0.125).astype(LOW)
    grad_q = jnp.einsum("bhqk,bkhd->bqhd", grad_low, heads_of(keys), preferred_element_type=FULL)
    grad_k = jnp.einsum("bhqk,bqhd->bkhd", grad_low, heads_of(queries), preferred_element_type=FULL)
    grad_v = jnp.einsum(
        "bhqk,bqhd->bkhd", shares.astype(LOW), grad_heads, preferred_element_type=FULL
    )
    return (
        grad_q.reshape(queries.shape).astype(LOW),
        grad_k.reshape(keys.shape).astype(LOW),
        grad_v.reshape(values.shape).astype(LOW),
    )


def adam(weight, first_moment, second, gradient, factor, fix_one, fix_two, decay):
    gradient = gradient * factor
    first_moment = BETA_ONE * first_moment + (1.0 - BETA_ONE) * gradient
    second = BETA_TWO * second + (1.0 - BETA_TWO) * gradient * gradient
    fixed_first = first_moment * fix_one
    fixed_second = second * fix_two
    weight = weight - LEARN_RATE * (
        fixed_first / (jnp.sqrt(fixed_second) + ADAM_EPS) + decay * weight
    )
    return (weight, first_moment, second)


def send(value, step, sources=None):
    groups = lax.axis_size("grp")
    sources = range(groups) if sources is None else sources
    return lax.ppermute(value, "grp", [(source, source ^ step) for source in sources])


def halves(value):
    middle = value.shape[1] // 2
    return value[:, :middle], value[:, middle:]


def assemble_kernel(value_ref, one_ref, left_ref, two_ref, right_ref, out_ref):
    rows, width = value_ref.shape
    middle = width // 2
    out_ref[:rows, :] = value_ref[...]
    out_ref[rows : 2 * rows, :middle] = one_ref[...]
    out_ref[2 * rows :, :middle] = left_ref[...]
    out_ref[rows : 2 * rows, middle:] = right_ref[:rows, :]
    out_ref[2 * rows : 3 * rows, middle:] = two_ref[...]
    out_ref[3 * rows :, middle:] = right_ref[rows:, :]


def gather_groups(value):
    rows, width = value.shape
    left, right = halves(value)
    left_one = send(left, 1)
    right_two = send(right, 2)
    left_more = send(jnp.concatenate([left, left_one], 0), 2)
    right_more = send(jnp.concatenate([right, right_two], 0), 1)
    return pl.pallas_call(
        assemble_kernel,
        out_shape=jax.ShapeDtypeStruct((4 * rows, width), value.dtype),
        cost_estimate=pl.CostEstimate(
            flops=0, bytes_accessed=8 * rows * width * value.dtype.itemsize, transcendentals=0
        ),
    )(value, left_one, left_more, right_two, right_more)


def reduce_groups(parts):
    rows = parts.shape[0] // 4
    left, right = halves(parts)
    left_low, right_low = left.astype(LOW), right.astype(LOW)
    got_left = send(left_low[2 * rows :], 2).astype(FULL)
    got_right = send(
        jnp.concatenate([right_low[rows : 2 * rows], right_low[3 * rows :]], 0), 1
    ).astype(FULL)
    more_left = send((left[rows : 2 * rows] + got_left[rows:]).astype(LOW), 1).astype(FULL)
    more_right = send((right[2 * rows : 3 * rows] + got_right[rows:]).astype(LOW), 2).astype(FULL)
    return jnp.concatenate(
        [left[:rows] + got_left[:rows] + more_left, right[:rows] + got_right[:rows] + more_right],
        1,
    )


def spread_last(value, is_last):
    last = lax.axis_size("grp") - 1
    left, right = halves(value)
    left_first = send(left, 1, [last])
    right_first = send(right, 2, [last])
    right_then = send(jnp.where(is_last, right, right_first), 1, [last, last ^ 2])
    left_then = send(jnp.where(is_last, left, left_first), 2, [last, last ^ 1])
    own = jnp.where(is_last, value, jnp.zeros_like(value))
    return own + jnp.concatenate([left_first + left_then, right_first + right_then], 1)


def collect_last(part):
    last = lax.axis_size("grp") - 1
    left, right = halves(part)
    left_first = send(left.astype(LOW), 2, [last ^ 3, last ^ 2]).astype(FULL)
    right_first = send(right.astype(LOW), 1, [last ^ 3, last ^ 1]).astype(FULL)
    left_then = send((left + left_first).astype(LOW), 1, [last ^ 1]).astype(FULL)
    right_then = send((right + right_first).astype(LOW), 2, [last ^ 2]).astype(FULL)
    return jnp.concatenate([left + left_first + left_then, right + right_first + right_then], 1)


def by_group(slots, group):
    return [
        lax.dynamic_index_in_dim(slots, group ^ source, 0, keepdims=False)
        for source in range(slots.shape[0])
    ]


def tie(value, *others):
    return lax.optimization_barrier((value,) + others)[0]


class Deal:
    def __init__(self, shard_rows, members, groups, group, member):
        self.rows = shard_rows
        self.members = members
        self.groups = groups
        self.group = group
        self.member = member
        self.round = groups * LANES
        self.blocks = shard_rows * members // LANES
        self.own = -(-self.blocks // groups)
        gap = self.round - shard_rows
        self.snug = gap > 0 and gap * members == LANES and self.own == members
        self.gap = gap if self.snug else 0

    def limit(self, block):
        return LANES - self.gap - self.gap * block

    def columns(self, feed_in):
        layers, rows, width = feed_in.shape
        groups, own, blocks = self.groups, self.own, self.blocks

        def kernel(group_ref, source_ref, before_ref, out_ref):
            place = pl.program_id(1) % own
            group = group_ref[0]
            lane = lax.broadcasted_iota(jnp.int32, out_ref.shape, 2)
            whole = jnp.logical_or(group != groups - 1, self.gap == 0)
            limit = jnp.where(whole, LANES, self.limit(place))
            limit = jnp.where(groups * place + group < blocks, limit, jnp.minimum(limit, 0))
            after = jnp.where(whole, LANES, self.limit(place) + self.gap)
            after = jnp.where(place > 0, after, LANES)
            kept = jnp.where(lane < limit, source_ref[...], 0.0)
            out_ref[...] = jnp.where(lane >= after, before_ref[...], kept).astype(LOW)

        def source_map(back):
            def index(layer, step, group_ref):
                block = groups * (step % own - back) + group_ref[0]
                block = jnp.clip(block, 0, blocks - 1)
                return (layer, 0, (step // own) * blocks + block)

            return index

        return pl.pallas_call(
            kernel,
            out_shape=jax.ShapeDtypeStruct((layers, rows, 2 * own * LANES), LOW),
            grid_spec=pltpu.PrefetchScalarGridSpec(
                num_scalar_prefetch=1,
                grid=(layers, 2 * own),
                in_specs=[
                    pl.BlockSpec((1, rows, LANES), source_map(0)),
                    pl.BlockSpec((1, rows, LANES), source_map(1)),
                ],
                out_specs=pl.BlockSpec((1, rows, LANES), lambda layer, step, ref: (layer, 0, step)),
            ),
        )(self.group.reshape(1), feed_in, feed_in)

    def gather(self, shard):
        width = shard.shape[1]
        if not self.snug:
            whole = lax.all_gather(shard, "dp", axis=0, tiled=True)
            padded = jnp.pad(whole, ((0, self.own * self.round - whole.shape[0]), (0, 0)))
            dealt = padded.reshape(self.own, self.groups, LANES, width)
            picked = lax.dynamic_index_in_dim(dealt, self.group, 1, keepdims=False)
            return picked.reshape(self.own * LANES, width)
        padded = jnp.pad(shard, ((0, self.gap), (0, 0)))
        doubled = jnp.concatenate([padded, padded], 0)
        start = self.gap * self.member + LANES * self.group
        piece = lax.dynamic_slice(doubled, (start, 0), (LANES, width))
        return lax.all_gather(piece, "dp", axis=0, tiled=True)

    def arrange(self, grad):
        if self.snug:
            return grad
        width = grad.shape[1]
        spread = jnp.zeros((self.own, self.groups, LANES, width), grad.dtype)
        spread = lax.dynamic_update_index_in_dim(
            spread, grad.reshape(self.own, 1, LANES, width), self.group, 1
        )
        return spread.reshape(-1, width)[: self.rows * self.members]

    def restore(self, parts):
        if not self.snug:
            return jnp.sum(parts, 0)
        width = parts.shape[2]
        line = parts.reshape(self.round, width)
        doubled = jnp.concatenate([line, line], 0)
        start = (self.round - self.gap * self.member) % self.round
        return lax.dynamic_slice(doubled, (start, 0), (self.rows, width))


def feed_in_step(weights, firsts, seconds, dealt, scalars, deal):
    layers, rows, width = weights.shape
    groups = dealt[0].shape[0]
    blocks = width // LANES
    half_blocks = blocks // 2
    own = dealt[0].shape[2] // (2 * LANES)
    dealt = jnp.stack(dealt)

    def whence(place, step):
        block = jnp.minimum(step * groups + place, blocks - 1)
        block = block - (block >= half_blocks).astype(jnp.int32) * half_blocks
        return block % groups, block // groups

    def kernel(group_ref, scalar_ref, w_ref, m_ref, v_ref, *rest):
        grads, outs = rest[: 2 * groups], rest[2 * groups :]
        lane = lax.broadcasted_iota(jnp.int32, (rows, LANES), 1)
        for place in range(groups):
            lanes = slice(place * LANES, (place + 1) * LANES)
            gradient = grads[place][0, 0].astype(FULL)
            if deal.gap:
                source, index = whence(place, pl.program_id(1))
                own_lanes = jnp.where(source == groups - 1, deal.limit(index), LANES)
                gradient = jnp.where(
                    lane < own_lanes, gradient, grads[groups + place][0, 0].astype(FULL)
                )
            new = adam(
                w_ref[0, :, lanes],
                m_ref[0, :, lanes],
                v_ref[0, :, lanes],
                gradient,
                scalar_ref[0],
                scalar_ref[1],
                scalar_ref[2],
                DECAY,
            )
            for out, value in zip(outs, new):
                out[0, :, lanes] = value

    def grad_spec(place, further):
        def index(layer, step, group_ref, scalar_ref):
            source, index = whence(place, step)
            part = (jnp.minimum(step * groups + place, blocks - 1) >= half_blocks).astype(jnp.int32)
            slot = jnp.bitwise_xor(group_ref[0], source)
            if further:
                index = jnp.where(source == groups - 1, jnp.minimum(index + 1, own - 1), 0)
            return (layer, slot, 0, part * own + index)

        return pl.BlockSpec((1, 1, rows, LANES), index)

    state_spec = pl.BlockSpec(
        (1, rows, groups * LANES), lambda layer, step, group_ref, scalar_ref: (layer, 0, step)
    )
    return pl.pallas_call(
        kernel,
        out_shape=[jax.ShapeDtypeStruct(weights.shape, FULL)] * 3,
        grid_spec=pltpu.PrefetchScalarGridSpec(
            num_scalar_prefetch=2,
            grid=(layers, -(-blocks // groups)),
            in_specs=[state_spec] * 3
            + [grad_spec(place, False) for place in range(groups)]
            + [grad_spec(place, True) for place in range(groups)],
            out_specs=[state_spec] * 3,
        ),
        cost_estimate=pl.CostEstimate(
            flops=20 * weights.size, bytes_accessed=26 * weights.size, transcendentals=weights.size
        ),
    )(deal.group.reshape(1), scalars, weights, firsts, seconds, *([dealt] * (2 * groups)))


def per_device(
    byte_tokens,
    seg_lengths,
    scripts,
    routes,
    step_count,
    attention_in,
    attention_out,
    feed_in,
    feed_out,
    embedding,
    norm_gains,
    first_attention_in,
    first_attention_out,
    first_feed_in,
    first_feed_out,
    first_embedding,
    first_norm_gains,
    second_attention_in,
    second_attention_out,
    second_feed_in,
    second_feed_out,
    second_embedding,
    second_norm_gains,
):
    groups = lax.axis_size("grp")
    members = lax.axis_size("dp")
    group = lax.axis_index("grp")
    member = lax.axis_index("dp")
    last = groups - 1
    is_decoder = group == last
    role = is_decoder.astype(jnp.int32)
    as_decoder = is_decoder.astype(FULL)
    decoder_slot = group ^ last
    micro, row_count = byte_tokens.shape[1:]
    tokens_here = micro * row_count
    shard_width = attention_in.shape[1]
    width = shard_width * members
    inner = attention_in.shape[2] // 3
    shard_inner = inner // members
    own_inner = inner // groups
    own_packed = 3 * own_inner
    own_width = width // groups
    shard_vocab = embedding.shape[0]
    vocab_size = shard_vocab * members
    capacity = 3 * row_count // (2 * members)
    slots = members * capacity
    deal = Deal(feed_out.shape[1], members, groups, group, member)
    scale_head = width ** (-0.5)

    tokens = byte_tokens[0]
    lengths = seg_lengths[0]
    bounds = jnp.cumsum(lengths, 1)
    position = jnp.arange(row_count, dtype=jnp.int32)
    segment = jnp.sum((position[None, :, None] >= bounds[:, None, :]).astype(jnp.int32), 2)
    same_row = segment[:, :, None] == segment[:, None, :]
    allowed_self = same_row & (
        jnp.logical_not(is_decoder) | (position[None, None, :] <= position[None, :, None])
    )
    starts = jnp.concatenate(
        [jnp.ones((micro, 1), bool), segment[:, 1:] != segment[:, :-1]], 1
    )
    previous = jnp.concatenate([jnp.zeros((micro, 1), jnp.int32), tokens[:, :-1]], 1)
    shifted = jnp.where(starts, 0, previous)
    inputs = jnp.where(is_decoder, shifted, tokens).reshape(tokens_here)
    target = routes[0, :, :, 0]
    hits = (target[:, :, None] == jnp.arange(members)[None, None, :]).astype(FULL)
    hits = hits * (1.0 - as_decoder)
    earlier = (position[:, None] > position[None, :]).astype(FULL)
    order = jnp.einsum("tu,bum->btm", earlier, hits, preferred_element_type=FULL)
    place = jnp.sum((order + capacity * jnp.arange(members, dtype=FULL)) * hits, 2)
    place = jnp.where(jnp.sum(hits, 2) > 0, place, -1.0)
    place = jnp.stack([place] + [send(place, step) for step in range(1, groups)])
    chosen = (
        place[..., None] == jnp.arange(slots, dtype=FULL)[None, None, None, :]
    ).astype(LOW)
    route_counts = jnp.sum(hits, 1)
    local_counts = (
        jnp.sum(
            jnp.where(scripts[0][..., None] == jnp.arange(3), lengths[..., None], 0), (0, 1)
        ).astype(FULL)
        * as_decoder
    )

    def pick(array):
        return lax.dynamic_index_in_dim(array, role, 0, keepdims=False).astype(LOW)

    def gather(value):
        return lax.all_gather(value, "dp", axis=0, tiled=True)

    def scatter(value):
        return lax.psum_scatter(value, "dp", scatter_dimension=0, tiled=True)

    extra = jnp.concatenate(
        [norm_gains.reshape(-1), local_counts, route_counts.reshape(-1)]
    ).astype(LOW)
    extra = jnp.pad(extra, (0, 8 * width - extra.shape[0])).reshape(8, width)
    packed_table = lax.all_gather(
        jnp.concatenate([embedding.astype(LOW), extra], 0), "dp", axis=0, tiled=False
    )
    table = packed_table[:, :shard_vocab].reshape(vocab_size, width)
    extras = packed_table[:, shard_vocab:].reshape(members, 8 * width)
    gain_size = 7 * shard_width
    gains = (
        extras[:, :gain_size].reshape(members, 7, shard_width).transpose(1, 0, 2).reshape(7, width)
    ).astype(FULL)
    counts = jnp.sum(extras[:, gain_size : gain_size + 3].astype(FULL), 0)
    scale_kind = 1.0 / (3.0 * jnp.maximum(counts, 1.0))
    came = extras[:, gain_size + 3 : gain_size + 3 + micro * members].astype(FULL)
    came = came.reshape(members, micro, members)
    came = lax.dynamic_index_in_dim(came, member, 2, keepdims=False)
    came = jnp.stack([came] + [send(came, step) for step in range(1, groups)])

    w_self_in = gather(pick(attention_in))

    onehot_inputs = (inputs[:, None] == jnp.arange(vocab_size)[None, :]).astype(LOW)
    stream0 = matmul(onehot_inputs, table)
    gain_self = jnp.where(is_decoder, gains[3], gains[0])
    normed_self = root_norm(stream0, gain_self).astype(LOW)
    packed_flat = matmul(normed_self, w_self_in).astype(LOW)
    w_self_out = gather(tie(pick(attention_out), table))
    dealt_in = deal.columns(tie(feed_in, table))
    w_enc_in = gather(dealt_in[0])
    packed = packed_flat.reshape(micro, row_count, 3 * inner)
    q_self, k_self, v_self = (
        packed[:, :, :inner],
        packed[:, :, inner : 2 * inner],
        packed[:, :, 2 * inner :],
    )
    attended_self, shares_self = attend(q_self, k_self, v_self, allowed_self)
    attended_self = attended_self.reshape(tokens_here, inner)
    w_enc_out = deal.gather(tie(feed_out[0].astype(LOW), packed_flat))
    stream1 = stream0 + matmul(attended_self, w_self_out)

    gain_next = jnp.where(is_decoder, gains[4], gains[1])
    normed_next = root_norm(stream1, gain_next).astype(LOW)
    all_next = gather_groups(normed_next)
    cross_in = attention_in[2].reshape(shard_width, 3, groups, own_inner)
    own_cross = lax.dynamic_index_in_dim(cross_in, group, 2, keepdims=False)
    own_cross = own_cross.reshape(shard_width, own_packed).astype(LOW)
    w_cross = gather(tie(own_cross, normed_next))
    w_query, w_memory = w_cross[:, :own_inner], w_cross[:, own_inner:]
    w_cross_out = gather(tie(attention_out[2].astype(LOW), normed_next))
    w_dec_in = gather(tie(dealt_in[1], all_next))
    hidden_enc = matmul(all_next, w_enc_in)
    gated_enc = gate_apply(hidden_enc).astype(LOW)
    w_dec_out = deal.gather(tie(feed_out[1].astype(LOW), gated_enc))
    stream2e = stream1 + reduce_groups(matmul(gated_enc, w_enc_out))
    states = root_norm(stream2e, gains[2]).astype(LOW)
    all_states = gather_groups(states)
    memory_rows = matmul(all_states, w_memory).astype(LOW)

    def enter(slot):
        return slot + (slot >= decoder_slot).astype(jnp.int32)

    def enter_back(slot):
        return slot - (decoder_slot < slot).astype(jnp.int32)

    def reorder(array, places):
        return jnp.stack(
            [lax.dynamic_index_in_dim(array, index, 0, keepdims=False) for index in places]
        )

    encoder_slots = [enter(slot) for slot in range(last)]
    placed = jnp.einsum(
        "gbts,gbtd->gbsd",
        reorder(chosen, encoder_slots),
        reorder(memory_rows.reshape(groups, micro, row_count, 2 * own_inner), encoder_slots),
        preferred_element_type=FULL,
    ).astype(LOW)
    outgoing = placed.reshape(last, micro, members, capacity, 2 * own_inner)
    outgoing = outgoing.transpose(2, 1, 0, 3, 4)
    outgoing = outgoing.reshape(members, micro * last * capacity, 2 * own_inner)
    arrived = lax.all_to_all(outgoing, "dp", split_axis=0, concat_axis=0, tiled=True)
    key_count = members * last * capacity
    memory = arrived.reshape(members, micro, last * capacity, 2 * own_inner)
    memory = memory.transpose(1, 0, 2, 3).reshape(micro, key_count, 2 * own_inner)
    present = (
        jnp.arange(capacity, dtype=FULL)[None, None, None, :]
        < reorder(came, encoder_slots).transpose(2, 1, 0)[..., None]
    ).reshape(micro, key_count)
    allowed_cross = jnp.broadcast_to(present[:, None, :], (micro, row_count, key_count))

    cross_input = lax.dynamic_index_in_dim(
        all_next.reshape(groups, tokens_here, width), decoder_slot, 0, keepdims=False
    )
    queries = matmul(cross_input, w_query).astype(LOW).reshape(micro, row_count, own_inner)
    keys, values = memory[:, :, :own_inner], memory[:, :, own_inner:]
    attended_own, shares_cross = attend(queries, keys, values, allowed_cross)
    attended_own = attended_own.reshape(tokens_here, own_inner)
    attended_cross = jnp.concatenate(
        [send(attended_own, last ^ source, [source]) for source in range(last)] + [attended_own],
        1,
    )
    stream2d = stream1 + matmul(attended_cross, w_cross_out)

    all_dec = spread_last(root_norm(stream2d, gains[5]).astype(LOW), is_decoder)
    hidden_dec = matmul(all_dec, w_dec_in)
    gated_dec = gate_apply(hidden_dec).astype(LOW)
    stream3 = stream2d + collect_last(matmul(gated_dec, w_dec_out))

    head_in = (root_norm(stream3, gains[6]) * scale_head).astype(LOW)
    logits = transposed_right(head_in, table)
    row_max = jnp.max(logits, -1, keepdims=True)
    raised = jnp.exp(logits - row_max)
    row_total = jnp.sum(raised, -1, keepdims=True)
    flat_tokens = tokens.reshape(tokens_here)
    onehot_vocab = (jnp.arange(vocab_size)[None, :] == flat_tokens[:, None]).astype(FULL)
    log_total = row_max[:, 0] + jnp.log(row_total[:, 0])
    picked = jnp.sum(logits * onehot_vocab, 1)
    token_kind = jnp.sum(
        jnp.where(
            segment[:, :, None] == jnp.arange(lengths.shape[1])[None, None, :],
            scripts[0][:, None, :],
            0,
        ),
        2,
    ).reshape(tokens_here)
    weight = jnp.sum(
        jnp.where(token_kind[:, None] == jnp.arange(3)[None, :], scale_kind[None, :], 0.0), 1
    )
    weight = weight * as_decoder
    loss_part = jnp.sum((log_total - picked) * weight)
    grad_logits = ((raised / row_total - onehot_vocab) * weight[:, None]).astype(LOW)
    cotangent, gain_six = root_norm_back(
        stream3, gains[6], matmul(grad_logits, table) * scale_head
    )

    def feed_back(hidden, grad_all, w_in, w_out):
        unused, pull = jax.vjp(gate_apply, hidden)
        grad_hidden = pull(transposed_right(grad_all, w_out))[0].astype(LOW)
        return grad_hidden, transposed_right(grad_hidden, w_in)

    grad_all_dec = spread_last(cotangent.astype(LOW), is_decoder)
    grad_hidden_dec, part = feed_back(hidden_dec, grad_all_dec, w_dec_in, w_dec_out)
    grad_dec_in = transposed_left(all_dec, grad_hidden_dec).astype(LOW)
    grad_dec_out = deal.arrange(transposed_left(gated_dec, grad_all_dec).astype(LOW))
    collected, grad_dec_in, grad_dec_out = lax.optimization_barrier(
        (collect_last(part), grad_dec_in, grad_dec_out)
    )
    owned_dec_in = scatter(grad_dec_in)
    owned_dec_out = scatter(grad_dec_out)
    grad_stream, gain_five = root_norm_back(stream2d, gains[5], collected)
    cotangent = cotangent + grad_stream

    grad_low = cotangent.astype(LOW)
    grad_attended = transposed_right(grad_low, w_cross_out).astype(LOW)
    grad_own = jnp.where(is_decoder, grad_attended[:, last * own_inner :], 0)
    for source in range(last):
        grad_own = grad_own + send(
            grad_attended[:, source * own_inner : (source + 1) * own_inner], last ^ source, [last]
        )
    grad_q, grad_k, grad_v = attend_back(
        queries, keys, values, shares_cross, grad_own.reshape(micro, row_count, own_inner)
    )
    grad_memory = jnp.concatenate([grad_k, grad_v], 2)
    grad_memory = grad_memory.reshape(micro, members, last * capacity, 2 * own_inner)
    grad_memory = grad_memory.transpose(1, 0, 2, 3).reshape(outgoing.shape)
    reached = lax.all_to_all(grad_memory, "dp", split_axis=0, concat_axis=0, tiled=True)
    grad_q = grad_q.reshape(tokens_here, own_inner)
    grad_query_in = transposed_left(cross_input, grad_q)
    collected = collect_last(transposed_right(grad_q, w_query))
    grad_cross_out = transposed_left(attended_cross, grad_low).astype(LOW)
    grad_table = transposed_left(grad_logits, head_in)
    reached, grad_query_in, grad_cross_out, collected, grad_table = lax.optimization_barrier(
        (reached, grad_query_in, grad_cross_out, collected, grad_table)
    )
    owned_cross_out = scatter(grad_cross_out)
    reached = reached.reshape(members, micro, last, capacity, 2 * own_inner)
    reached = reached.transpose(2, 1, 0, 3, 4).reshape(last, micro, slots, 2 * own_inner)
    grad_rows = jnp.einsum(
        "gbts,gbsd->gbtd",
        chosen,
        reorder(reached, [jnp.minimum(enter_back(slot), last - 1) for slot in range(groups)]),
        preferred_element_type=FULL,
    )
    grad_rows = grad_rows.astype(LOW).reshape(groups * tokens_here, 2 * own_inner)
    grad_stream, gain_four = root_norm_back(stream1, gains[4], collected)
    cotangent_dec = cotangent + grad_stream

    reduced = reduce_groups(transposed_right(grad_rows, w_memory))
    grad_memory_in = transposed_left(all_states, grad_rows)
    reduced, grad_cross_in, owned_dec_in, owned_dec_out = lax.optimization_barrier(
        (
            reduced,
            jnp.concatenate([grad_query_in, grad_memory_in], 1),
            owned_dec_in,
            owned_dec_out,
        )
    )
    owned_cross_in = scatter(grad_cross_in)
    cotangent_enc, gain_two = root_norm_back(stream2e, gains[2], reduced)
    grad_low = jnp.where(is_decoder, 0.0, cotangent_enc).astype(LOW)
    grad_all_enc = gather_groups(grad_low)
    grad_hidden_enc, part = feed_back(hidden_enc, grad_all_enc, w_enc_in, w_enc_out)
    grad_enc_in = transposed_left(all_next, grad_hidden_enc).astype(LOW)
    grad_enc_out = deal.arrange(transposed_left(gated_enc, grad_all_enc).astype(LOW))
    reduced, grad_enc_in, grad_enc_out, owned_cross_in, owned_cross_out = (
        lax.optimization_barrier(
            (reduce_groups(part), grad_enc_in, grad_enc_out, owned_cross_in, owned_cross_out)
        )
    )
    owned_enc_in = scatter(grad_enc_in)
    owned_enc_out = scatter(grad_enc_out)
    grad_stream, gain_one = root_norm_back(stream1, gains[1], reduced)
    cotangent_enc = cotangent_enc + grad_stream

    cotangent = jnp.where(is_decoder, cotangent_dec, cotangent_enc)
    grad_low = cotangent.astype(LOW)
    grad_attended = transposed_right(grad_low, w_self_out).astype(LOW)
    grads = attend_back(
        q_self, k_self, v_self, shares_self, grad_attended.reshape(micro, row_count, inner)
    )
    grad_packed = jnp.concatenate(grads, 2).reshape(tokens_here, 3 * inner)
    grad_stream, gain_zero = root_norm_back(
        stream0, gain_self, transposed_right(grad_packed, w_self_in)
    )
    cotangent = cotangent + grad_stream
    grad_lookup = lax.dot_general(
        onehot_inputs.astype(FULL),
        cotangent,
        (((0,), (0,)), ((), ())),
        precision=lax.Precision.HIGHEST,
        preferred_element_type=FULL,
    )
    grad_table = grad_table + grad_lookup

    all_normed, all_attended = (
        gather_groups(tie(normed_self, all_next)),
        gather_groups(tie(attended_self, all_next)),
    )

    def exchange_columns(value, columns):
        pieces = jnp.stack(
            [value[:, start : start + columns] for start in range(0, groups * columns, columns)]
        )
        mine = by_group(pieces, group)
        return jnp.concatenate(
            [mine[0]] + [send(mine[step], step) for step in range(1, groups)], 0
        )

    slot_of = (jnp.arange(groups * tokens_here) // tokens_here)[:, None]
    from_encoder = slot_of != decoder_slot

    def both_roles(left, right):
        right_slots = right.reshape(groups, tokens_here, -1)
        left_slots = left.reshape(groups, tokens_here, -1)
        return (
            transposed_left(left, jnp.where(from_encoder, right, 0)),
            transposed_left(
                lax.dynamic_index_in_dim(left_slots, decoder_slot, 0, keepdims=False),
                lax.dynamic_index_in_dim(right_slots, decoder_slot, 0, keepdims=False),
            ),
        )

    self_in_enc, self_in_dec = both_roles(all_normed, exchange_columns(grad_packed, own_packed))
    self_out_enc, self_out_dec = both_roles(all_attended, exchange_columns(grad_low, own_width))
    self_out = jnp.stack(
        [
            self_out_enc.reshape(members, shard_inner, own_width),
            self_out_dec.reshape(members, shard_inner, own_width),
        ],
        1,
    ).reshape(width, own_width)
    owned_self = scatter(
        tie(jnp.concatenate([self_in_enc, self_in_dec, self_out], 1), owned_enc_in, owned_enc_out)
    )

    encoder_only = 1.0 - as_decoder
    grad_gains = jnp.stack(
        [
            gain_zero * encoder_only,
            gain_one * encoder_only,
            gain_two * encoder_only,
            gain_zero * as_decoder,
            gain_four * as_decoder,
            gain_five * as_decoder,
            gain_six * as_decoder,
        ]
    )
    gain_rows = grad_gains.reshape(7, members, shard_width).transpose(1, 0, 2)
    gain_rows = gain_rows.reshape(members, gain_size)
    scalars = jnp.concatenate([loss_part[None], local_counts])
    gain_rows = jnp.concatenate(
        [gain_rows, jnp.broadcast_to(scalars[None], (members, 4))], 1
    )
    gain_rows = jnp.pad(gain_rows, ((0, 0), (0, 8 * width - gain_rows.shape[1])))
    last_pack = jnp.concatenate(
        [
            grad_table.reshape(members, shard_vocab, width),
            gain_rows.reshape(members, 8, width),
        ],
        1,
    )
    owned_pack = scatter(tie(last_pack.reshape(members * (shard_vocab + 8), width), owned_self))

    def every(value):
        return gather_groups(value).reshape((groups,) + value.shape)

    every_dec_in, every_dec_out = every(owned_dec_in), every(owned_dec_out)
    every_enc_in, every_enc_out = every(owned_enc_in), every(owned_enc_out)
    summed_pack = sum(by_group(every(owned_pack), group))
    grad_embedding = summed_pack[:shard_vocab]
    summed_rest = summed_pack[shard_vocab:].reshape(-1)
    grad_norm_gains = summed_rest[:gain_size].reshape(7, shard_width)
    loss_value = summed_rest[gain_size]
    total_counts = summed_rest[gain_size + 1 : gain_size + 4]
    cross_parts = by_group(every(owned_cross_in), group)
    self_parts = by_group(every(owned_self), group)
    final_cross_out = spread_last(owned_cross_out, is_decoder).astype(FULL)
    final_attention_in = jnp.stack(
        [
            jnp.concatenate([part[:, :own_packed] for part in self_parts], 1),
            jnp.concatenate([part[:, own_packed : 2 * own_packed] for part in self_parts], 1),
            jnp.concatenate(
                [
                    part[:, own_inner * kind : own_inner * (kind + 1)]
                    for kind in range(3)
                    for part in cross_parts
                ],
                1,
            ),
        ]
    )
    final_attention_out = jnp.stack(
        [
            jnp.concatenate([part[:shard_inner, 2 * own_packed :] for part in self_parts], 1),
            jnp.concatenate([part[shard_inner:, 2 * own_packed :] for part in self_parts], 1),
            final_cross_out,
        ]
    )
    final_feed_out = jnp.stack(
        [
            deal.restore(jnp.stack(by_group(parts, group)))
            for parts in (every_enc_out, every_dec_out)
        ]
    ).astype(FULL)

    def square(value):
        value = value.astype(FULL)
        return jnp.sum(value * value)

    first_group = (group == 0).astype(FULL)
    squares = (
        square(owned_enc_in)
        + square(owned_dec_in)
        + square(owned_enc_out)
        + square(owned_dec_out)
        + square(owned_cross_in)
        + square(owned_self)
        + as_decoder * square(owned_cross_out)
        + first_group * (square(grad_embedding) + square(grad_norm_gains))
    )
    squares = squares.reshape(1)
    for step in (1, 2):
        squares = squares + send(squares, step)
    step = 1
    while step < members:
        pairs = [(source, source ^ step) for source in range(members)]
        squares = squares + lax.ppermute(squares, "dp", pairs)
        step *= 2
    norm = jnp.sqrt(squares[0])
    factor = jnp.minimum(1.0, CLIP / (norm + 1e-06))
    step_value = step_count[0].astype(FULL)
    fix_one = 1.0 / (1.0 - BETA_ONE**step_value)
    fix_two = 1.0 / (1.0 - BETA_TWO**step_value)
    new_feed_in = feed_in_step(
        feed_in,
        first_feed_in,
        second_feed_in,
        (every_enc_in, every_dec_in),
        jnp.stack([factor, fix_one, fix_two]),
        deal,
    )

    def step(weight, first, second, gradient, decay):
        return adam(weight, first, second, gradient, factor, fix_one, fix_two, decay)

    results = [
        step(attention_in, first_attention_in, second_attention_in, final_attention_in, DECAY),
        step(attention_out, first_attention_out, second_attention_out, final_attention_out, DECAY),
        new_feed_in,
        step(feed_out, first_feed_out, second_feed_out, final_feed_out, DECAY),
        step(embedding, first_embedding, second_embedding, grad_embedding, DECAY),
        step(norm_gains, first_norm_gains, second_norm_gains, grad_norm_gains, 0.0),
    ]
    return (
        *(result[0] for result in results),
        *(result[1] for result in results),
        *(result[2] for result in results),
        loss_value,
        total_counts,
        norm,
    )


def solution(mesh):
    weights = (
        P(None, "dp", None),
        P(None, "dp", None),
        P(None, "dp", None),
        P(None, "dp", None),
        P("dp", None),
        P(None, "dp"),
    )
    in_specs = (
        P(("grp", "dp"), None, None),
        P(("grp", "dp"), None, None),
        P(("grp", "dp"), None, None),
        P(("grp", "dp"), None, None, None),
        P(),
    ) + 3 * weights
    out_specs = 3 * weights + (P(), P(), P())
    return jax.shard_map(
        per_device, mesh=mesh, in_specs=in_specs, out_specs=out_specs, check_vma=False
    )
```
